32 devices in a mesh: section: 2 (over x), tile: 16 (over z, y, core).
Axes of the slice: x: 2, y: 2, z: 4, core: 2. Of those that a mesh axis runs over, the one named last changes fastest.
Arguments:
- queries: bfloat16 [2, 8192, 3072], P('section', 'tile')
- key_values: bfloat16 [2, 2, 8192, 3072], P(None, 'section', 'tile')
- neighbours: int32 [64, 8], P('tile'), may hold values from 0 to 63, as said below
- clean_section: int32 [64], P('tile'), may hold values from 0 to 1
Outputs:
- attended: bfloat16 [2, 8192, 3072], P('section', 'tile')
The draws below stay inside these ranges and needn't reach their ends.
Inputs may be any that keep to these rules, and one draw needn't show every extreme that they name: neighbours[t] names 8 distinct tiles of the span; the first is t itself; all lie on the device that holds t or on the two devices next to it along the closed cycle of tile devices, and every list names a tile of each of those two devices.
All inputs are finite; a program needn't handle non-finite values.
Results may differ from the reference program's by a relative error of at most 0.0047.
Values may be sent and summed in bfloat16 or wider, within the bound.
No kernel may reach another device: no remote copies, remote signals or barrier semaphores. Data moves between devices by JAX's collectives and lax.ppermute only.
A program may use at most 192 MiB of HBM per device.

```python
import jax
import jax.numpy as jnp
from jax import lax

HEADS = 24
HEAD = 128
TILE = 128
NB = 8
TILES_DEV = 4
FEAT = 3072
TILES = 64
SPAN_TOK = 8192
N_SECTION = 2


def key_base(key):
    return jnp.clip(jax.random.normal(jax.random.fold_in(key, 101), (N_SECTION, SPAN_TOK, HEADS * HEAD), jnp.float32), -4.0, 4.0)


def draw_key_values(key, part):
    keys_part = key_base(key)
    shape_all = (N_SECTION, SPAN_TOK, HEADS * HEAD)
    values_part = jnp.clip(jax.random.normal(jax.random.fold_in(key, 102), shape_all, jnp.float32), -4.0, 4.0)
    return jnp.stack([keys_part, values_part], 0).astype(jnp.bfloat16)


def draw_queries(key, part):
    shape_all = (N_SECTION, SPAN_TOK, HEADS * HEAD)
    queries_part = jnp.clip(jax.random.normal(jax.random.fold_in(key, 103), shape_all, jnp.float32), -4.0, 4.0)
    return queries_part.astype(jnp.bfloat16)


def draw_neighbours(key, part):
    tile_ids = jnp.arange(TILES)[:, None]
    device_ids = tile_ids // TILES_DEV
    local_ids = tile_ids % TILES_DEV
    candidate = jnp.arange(3 * TILES_DEV)[None, :]
    ranking = jax.random.randint(key, (TILES, 3 * TILES_DEV), 0, 2 ** 20) * (3 * TILES_DEV) + candidate
    ranking = jnp.where(candidate == TILES_DEV + local_ids, -3, ranking)
    ranking = jnp.where(candidate == local_ids, -2, ranking)
    ranking = jnp.where(candidate == 2 * TILES_DEV + local_ids, -1, ranking)
    chosen = jnp.argsort(ranking, axis=1)[:, :NB]
    cycle_size = TILES // TILES_DEV
    source_device = (device_ids - 1 + chosen // TILES_DEV) % cycle_size
    return (source_device * TILES_DEV + chosen % TILES_DEV).astype(jnp.int32)


def place_ends(array, own_key, smallest, largest):
    longest = array.shape.index(max(array.shape))
    spots = []
    for shift in (0, 1):
        where = [jax.random.randint(jax.random.fold_in(own_key, axis), (), 0, length) for axis, length in enumerate(array.shape)]
        where[longest] = (where[longest] + shift) % array.shape[longest]
        spots.append(tuple(where))
    return array.at[spots[0]].set(smallest).at[spots[1]].set(largest)


def setup_inputs(seed: int = 0) -> dict:
    streams_of = jax.random.split(jax.random.key(seed), 5)
    queries = draw_queries(jax.random.fold_in(streams_of[4], 71), 0)
    key_values = draw_key_values(jax.random.fold_in(streams_of[4], 71), 0)
    neighbours = draw_neighbours(jax.random.fold_in(streams_of[4], 71), 0)
    clean_section = place_ends(jax.random.randint(streams_of[3], (TILES,), 0, N_SECTION), jax.random.fold_in(streams_of[3], 1), 0, N_SECTION - 1).astype(jnp.int32)
    return {"queries": queries, "key_values": key_values, "neighbours": neighbours, "clean_section": clean_section}


def reference(queries, key_values, neighbours, clean_section):
    score_scale = HEAD ** -0.5
    kv_tiles = key_values.reshape(2, N_SECTION, TILES, TILE, HEADS, HEAD)
    span_outputs = []
    for section_id in range(N_SECTION):
        query_tiles = queries[section_id].reshape(TILES, TILE, HEADS, HEAD)
        keys_own = kv_tiles[0, section_id]
        values_own = kv_tiles[1, section_id]

        def one_tile(tile_args):
            query_tile, listed, clean_index = tile_args
            cache_pair = lax.dynamic_index_in_dim(kv_tiles, clean_index, 1, keepdims=False)
            live_cache = clean_index != section_id
            live_mask = jnp.concatenate([jnp.ones((NB * TILE,), bool), jnp.broadcast_to(live_cache, (NB * TILE,))])
            keys_list = jnp.concatenate([keys_own[listed], cache_pair[0][listed]], 0).reshape(2 * NB * TILE, HEADS, HEAD).astype(jnp.float32)
            values_list = jnp.concatenate([values_own[listed], cache_pair[1][listed]], 0).reshape(2 * NB * TILE, HEADS, HEAD).astype(jnp.float32)
            scores = jnp.einsum('qhd,khd->hqk', query_tile.astype(jnp.float32), keys_list, precision=lax.Precision.HIGHEST) * score_scale
            scores = jnp.where(live_mask[None, None, :], scores, -1e30)
            maxima = jnp.max(scores, axis=-1, keepdims=True)
            weights = jnp.exp(scores - maxima)
            totals = jnp.sum(weights, axis=-1)
            rounded = lax.optimization_barrier(weights.astype(jnp.bfloat16)).astype(jnp.float32)
            result = jnp.einsum('hqk,khd->qhd', rounded, values_list, precision=lax.Precision.HIGHEST)
            result = result / jnp.transpose(totals, (1, 0))[..., None]
            return result.astype(jnp.bfloat16)

        results = lax.map(one_tile, (query_tiles, neighbours, clean_section.astype(jnp.int32)))
        span_outputs.append(results.reshape(SPAN_TOK, FEAT))
    return jnp.stack(span_outputs, 0)
```

```python
import functools
import math

import jax
import jax.numpy as jnp
from jax import lax
from jax.experimental import pallas as pl
from jax.experimental.pallas import tpu as pltpu
from jax.sharding import PartitionSpec as P

HEAD = 128
TILE = 128
LOG2E = math.log2(math.e)
MASKED = -1e30 * LOG2E
SIZES = (3, 4, 4, 4, 4, 3, 2)


def group_sizes(heads):
    if sum(SIZES) == heads:
        return SIZES
    return (heads,) if heads < 4 else (4,) * (heads // 4) + ((heads % 4,) if heads % 4 else ())


def parts_of(x):
    hi = x.astype(jnp.bfloat16).astype(jnp.float32)
    rest = x - hi
    mid = rest.astype(jnp.bfloat16).astype(jnp.float32)
    return hi, mid, rest - mid


def attend_kernel(
    slots_ref, dead_ref, q_ref, qp_ref, own_ref, even_ref, odd_ref,
    out_ref, stat_ref, msg_ref, keys, values, scores, *, tiles, listed, heads, scale,
):
    head = pl.program_id(0)
    columns = pl.ds(pl.multiple_of(head * HEAD, HEAD), HEAD)
    for region, ref in enumerate((own_ref, even_ref, odd_ref)):
        for tile in range(tiles):
            rows = slice(tile * TILE, (tile + 1) * TILE)
            keys[region * tiles + tile] = ref[0, rows, :]
            values[region * tiles + tile] = ref[1, rows, :]
    lane = lax.broadcasted_iota(jnp.int32, (TILE, HEAD), 1)

    @pl.when(head == 0)
    def _():
        stat_ref[...] = jnp.zeros_like(stat_ref)
        msg_ref[:, heads * HEAD :] = jnp.zeros((tiles * TILE, HEAD), msg_ref.dtype)

    def run(tile, query, masked_rows):
        count = query.shape[0]
        base = tile * listed

        def pair(ref, index):
            first = ref[slots_ref[base + 2 * index]]
            second = ref[slots_ref[base + 2 * index + 1]]
            return jnp.concatenate([first, second], 0)

        running = None
        for index in range(listed // 2):
            part = lax.dot_general(
                query, pair(keys, index), (((1,), (1,)), ((), ())),
                preferred_element_type=jnp.float32,
            )
            scores[:count, 2 * index * TILE : 2 * (index + 1) * TILE] = part
            larger = jnp.maximum(part[:, :TILE], part[:, TILE:])
            running = larger if running is None else jnp.maximum(running, larger)
        top = jnp.max(running, axis=1, keepdims=True) * scale
        extra = None
        if masked_rows:
            own_row = lax.broadcasted_iota(jnp.int32, (count, 1), 0) < masked_rows
            top = jnp.where(own_row, jnp.maximum(top, MASKED), top)
            extra = jnp.where(own_row, jnp.exp2(MASKED - top), 0.0)
        total = None
        acc = None
        for index in range(listed // 2):
            part = scores[:count, 2 * index * TILE : 2 * (index + 1) * TILE]
            weight = jnp.exp2(part * scale - top)
            if extra is not None:
                weight = weight + extra
            halves = weight[:, :TILE] + weight[:, TILE:]
            total = halves if total is None else total + halves
            term = lax.dot_general(
                weight.astype(jnp.bfloat16), pair(values, index), (((1,), (0,)), ((), ())),
                preferred_element_type=jnp.float32,
            )
            acc = term if acc is None else acc + term
        total = jnp.sum(total, axis=1, keepdims=True)
        return (acc / total).astype(jnp.bfloat16), top, total

    def one_tile(tile, carry):
        rows = pl.ds(pl.multiple_of(tile * TILE, TILE), TILE)

        @pl.when(dead_ref[tile] == 1)
        def _():
            query = jnp.concatenate([q_ref[rows, :], qp_ref[rows, :]], 0)
            result, top, total = run(tile, query, TILE)
            out_ref[rows, :] = result[:TILE]
            msg_ref[rows, columns] = result[TILE:]
            stats = msg_ref[rows, heads * HEAD :].astype(jnp.float32)
            for k, value in enumerate((*parts_of(top[TILE:]), *parts_of(total[TILE:]))):
                stats = jnp.where(lane == head * 6 + k, value, stats)
            msg_ref[rows, heads * HEAD :] = stats.astype(jnp.bfloat16)

        @pl.when(dead_ref[tile] == 0)
        def _():
            result, top, total = run(tile, q_ref[rows, :], 0)
            out_ref[rows, :] = result
            msg_ref[rows, columns] = jnp.zeros((TILE, HEAD), jnp.bfloat16)
            stats = stat_ref[rows, :]
            stats = jnp.where(lane == head * 2, top, stats)
            stat_ref[rows, :] = jnp.where(lane == head * 2 + 1, total, stats)

        return carry

    lax.fori_loop(0, tiles, one_tile, 0)


def merge_kernel(dead_ref, own_ref, stat_ref, msg_ref, other_ref, *rest, tiles):
    out_ref = rest[-1]
    head = pl.program_id(0)
    lane = lax.broadcasted_iota(jnp.int32, (TILE, HEAD), 1)

    def pick(stats, index):
        return jnp.sum(jnp.where(lane == index, stats, 0.0), axis=1, keepdims=True)

    for tile in range(tiles):
        rows = slice(tile * TILE, (tile + 1) * TILE)

        @pl.when(dead_ref[tile] == 1)
        def _():
            out_ref[rows, :] = own_ref[rows, :]

        @pl.when(dead_ref[tile] == 0)
        def _():
            stats = stat_ref[rows, :]
            others = other_ref[rows, :].astype(jnp.float32)
            top, total = pick(stats, head * 2), pick(stats, head * 2 + 1)
            values = [pick(others, head * 6 + k) for k in range(6)]
            top_o = values[0] + values[1] + values[2]
            total_o = values[3] + values[4] + values[5]
            most = jnp.maximum(top, top_o)
            weight = total * jnp.exp2(top - most)
            weight_o = total_o * jnp.exp2(top_o - most)
            sum_of = weight + weight_o
            result = own_ref[rows, :].astype(jnp.float32) * (weight / sum_of)
            result = result + msg_ref[rows, :].astype(jnp.float32) * (weight_o / sum_of)
            out_ref[rows, :] = result.astype(out_ref.dtype)


def local(queries, key_values, neighbours, clean_section):
    tok_dev, feat = queries.shape[1:]
    tiles = tok_dev // TILE
    listed = neighbours.shape[1]
    heads = feat // HEAD
    cycle = lax.axis_size("tile")
    here = lax.axis_index("tile")
    section = lax.axis_index("section")
    scale = HEAD ** (-0.5) * LOG2E

    query = queries[0]
    own = key_values[:, 0]
    dead = (clean_section == section).astype(jnp.int32)
    device = neighbours // tiles
    region = jnp.where(device == here, 0, jnp.where(device == here + 1 - 2 * (here % 2), 1, 2))
    slots = (region * tiles + neighbours % tiles).reshape(-1)

    even_pairs = [(i, i ^ 1) for i in range(cycle)]
    odd_pairs = [(i, (i + 1) % cycle if i % 2 else (i - 1) % cycle) for i in range(cycle)]
    swap = [(0, 1), (1, 0)]

    even = lax.ppermute(own, "tile", even_pairs)

    sizes = group_sizes(heads)
    starts = [sum(sizes[:g]) for g in range(len(sizes))]
    odd, partner = [], []
    for start, size in zip(starts, sizes):
        low, high = start * HEAD, (start + size) * HEAD
        odd.append(lax.ppermute(own[:, :, low:high], "tile", odd_pairs))
        partner.append(lax.ppermute(query[:, low:high], "section", swap))

    def attend(start, size, odd_part, partner_part):
        units = size * tiles * 2 * TILE * listed * TILE
        return pl.pallas_call(
            functools.partial(
                attend_kernel, tiles=tiles, listed=listed, heads=size, scale=scale
            ),
            grid_spec=pltpu.PrefetchScalarGridSpec(
                num_scalar_prefetch=2,
                grid=(size,),
                in_specs=[
                    pl.BlockSpec((tok_dev, HEAD), lambda h, *_: (0, start + h)),
                    pl.BlockSpec((tok_dev, HEAD), lambda h, *_: (0, h)),
                    pl.BlockSpec((2, tok_dev, HEAD), lambda h, *_: (0, 0, start + h)),
                    pl.BlockSpec((2, tok_dev, HEAD), lambda h, *_: (0, 0, start + h)),
                    pl.BlockSpec((2, tok_dev, HEAD), lambda h, *_: (0, 0, h)),
                ],
                out_specs=[
                    pl.BlockSpec((tok_dev, HEAD), lambda h, *_: (0, h)),
                    pl.BlockSpec((tok_dev, HEAD), lambda h, *_: (0, 0)),
                    pl.BlockSpec((tok_dev, (size + 1) * HEAD), lambda h, *_: (0, 0)),
                ],
                scratch_shapes=[
                    pltpu.VMEM((3 * tiles, TILE, HEAD), jnp.bfloat16),
                    pltpu.VMEM((3 * tiles, TILE, HEAD), jnp.bfloat16),
                    pltpu.VMEM((2 * TILE, listed * TILE), jnp.float32),
                ],
            ),
            out_shape=[
                jax.ShapeDtypeStruct((tok_dev, size * HEAD), jnp.bfloat16),
                jax.ShapeDtypeStruct((tok_dev, HEAD), jnp.float32),
                jax.ShapeDtypeStruct((tok_dev, (size + 1) * HEAD), jnp.bfloat16),
            ],
            cost_estimate=pl.CostEstimate(
                flops=4 * units * HEAD, transcendentals=units,
                bytes_accessed=size * HEAD * tok_dev * 2 * 10,
            ),
            compiler_params=pltpu.CompilerParams(
                dimension_semantics=("arbitrary",), vmem_limit_bytes=24 << 20
            ),
            name="attend",
        )(slots, dead, query, partner_part, own, even, odd_part)

    def merge(start, size, mine, stats, message, target):
        block = pl.BlockSpec((tok_dev, HEAD), lambda h, *_: (0, h))
        last = [] if target is None else [target]
        return pl.pallas_call(
            functools.partial(merge_kernel, tiles=tiles),
            grid_spec=pltpu.PrefetchScalarGridSpec(
                num_scalar_prefetch=1,
                grid=(size,),
                in_specs=[
                    block,
                    pl.BlockSpec((tok_dev, HEAD), lambda h, *_: (0, 0)),
                    block,
                    pl.BlockSpec((tok_dev, HEAD), lambda h, *_: (0, size)),
                ]
                + [pl.BlockSpec(memory_space=pl.ANY)] * len(last),
                out_specs=pl.BlockSpec((tok_dev, HEAD), lambda h, *_: (0, start + h)),
            ),
            out_shape=jax.ShapeDtypeStruct((tok_dev, feat), jnp.bfloat16),
            input_output_aliases={5: 0} if last else {},
            cost_estimate=pl.CostEstimate(
                flops=size * HEAD * tok_dev * 8, transcendentals=0,
                bytes_accessed=size * HEAD * tok_dev * 2 * 3,
            ),
            compiler_params=pltpu.CompilerParams(
                dimension_semantics=("arbitrary",), vmem_limit_bytes=16 << 20
            ),
            name="merge",
        )(dead, mine, stats, message, message, *last)

    target = None
    for g, (start, size) in enumerate(zip(starts, sizes)):
        mine, stats, message = attend(start, size, odd[g], partner[g])
        message = lax.ppermute(message, "section", swap)
        target = merge(start, size, mine, stats, message, target)
    return target[None]


def solution(mesh):
    placed = (
        P("section", "tile", None),
        P(None, "section", "tile", None),
        P("tile", None),
        P("tile"),
    )
    return jax.shard_map(
        local, mesh=mesh, in_specs=placed, out_specs=P("section", "tile", None), check_vma=False
    )
```

```python
import functools
import math

import jax
import jax.numpy as jnp
from jax import lax
from jax.experimental import pallas as pl
from jax.experimental.pallas import tpu as pltpu
from jax.sharding import PartitionSpec as P

HEAD = 128
TILE = 128
LOG2E = math.log2(math.e)
MASKED = -1e30 * LOG2E
LOWEST = -3e38
SPAN = 4
LANES = 16
SIZES = (4, 4, 4, 4, 4, 2, 1, 1)
DEPTH = 2
LAG = 2


def group_sizes(heads):
    if sum(SIZES) == heads:
        return SIZES
    return (4,) * (heads // 4) + (1,) * (heads % 4)


def parts_of(x):
    hi = x.astype(jnp.bfloat16).astype(jnp.float32)
    rest = x - hi
    mid = rest.astype(jnp.bfloat16).astype(jnp.float32)
    return hi, mid, rest - mid


def attend_kernel(
    slots_ref, dead_ref, q_ref, qp_ref, own_ref, even_ref, odd_ref,
    out_ref, stat_ref, msg_ref, windows, scores, sems,
    *, tiles, listed, heads, start, scale,
):
    head = pl.program_id(0)
    slot = head % 2
    columns = pl.ds(pl.multiple_of(head * HEAD, HEAD), HEAD)
    lane = lax.broadcasted_iota(jnp.int32, (TILE, HEAD), 1)
    own_row = lax.broadcasted_iota(jnp.int32, (2 * TILE, 1), 0) < TILE
    count = listed // SPAN
    wide = SPAN * TILE

    def copies(which):
        for region, ref in enumerate((own_ref, even_ref, odd_ref)):
            first = (which if region == 2 else start + which) * HEAD
            yield pltpu.make_async_copy(
                ref.at[:, :, :, pl.ds(pl.multiple_of(first, HEAD), HEAD)],
                windows.at[which % 2, :, region * tiles : (region + 1) * tiles],
                sems.at[which % 2, region],
            )

    @pl.when(head == 0)
    def _():
        for copy in copies(head):
            copy.start()
        stat_ref[...] = jnp.zeros_like(stat_ref)

    @pl.when(head + 1 < heads)
    def _():
        for copy in copies(head + 1):
            copy.start()

    for copy in copies(head):
        copy.wait()

    def rows_of(tile):
        return slice(tile * TILE, (tile + 1) * TILE)

    def gathered(kind, tile, index):
        first = tile * listed + SPAN * index
        return jnp.concatenate(
            [windows[slot, kind, slots_ref[first + k]] for k in range(SPAN)], 0
        )

    def score(tile, index, query, running):
        part = lax.dot_general(
            query, gathered(0, tile, index), (((1,), (1,)), ((), ())),
            preferred_element_type=jnp.float32,
        )
        scores[tile % 2, :, wide * index : wide * (index + 1)] = part
        for k in range(SPAN):
            piece = part[:, k * TILE : (k + 1) * TILE]
            running = piece if running is None else jnp.maximum(running, piece)
        return running

    def query_of(tile):
        return jnp.concatenate([q_ref[rows_of(tile), :], qp_ref[rows_of(tile), :]], 0)

    running = None
    query = query_of(0)
    for index in range(count):
        running = score(0, index, query, running)
    for tile in range(tiles):
        rows = rows_of(tile)
        floor = jnp.where(own_row & (dead_ref[tile] == 1), MASKED, LOWEST)
        top = jnp.maximum(jnp.max(running, axis=1, keepdims=True) * scale, floor)
        extra = jnp.where(floor == LOWEST, 0.0, jnp.exp2(floor - top))
        running, total, acc = None, None, None
        if tile + 1 < tiles:
            query = query_of(tile + 1)
        for index in range(count):
            if tile + 1 < tiles:
                running = score(tile + 1, index, query, running)
            part = scores[tile % 2, :, wide * index : wide * (index + 1)]
            weight = jnp.exp2(part * scale - top) + extra
            for k in range(SPAN):
                piece = weight[:, k * TILE : (k + 1) * TILE]
                total = piece if total is None else total + piece
            term = jnp.dot(
                weight.astype(jnp.bfloat16), gathered(1, tile, index),
                preferred_element_type=jnp.float32,
            )
            acc = term if acc is None else acc + term
        total = jnp.sum(total, axis=1, keepdims=True)
        result = (acc * (1.0 / total)).astype(jnp.bfloat16)
        out_ref[rows, :] = result[:TILE]
        msg_ref[rows, columns] = result[TILE:]
        stats = stat_ref[rows, :]
        for k, value in enumerate((top[:TILE], total[:TILE], top[TILE:], total[TILE:])):
            stats = jnp.where(lane == head + LANES * k, value, stats)
        stat_ref[rows, :] = stats

    @pl.when(head == heads - 1)
    def _():
        for tile in range(tiles):
            rows = rows_of(tile)
            packed = jnp.zeros((TILE, HEAD), jnp.float32)
            for k, value in enumerate(parts_of(stat_ref[rows, :])):
                moved = pltpu.roll(value, (HEAD - 2 * LANES + 2 * LANES * k) % HEAD, 1)
                packed = jnp.where(lane // (2 * LANES) == k, moved, packed)
            msg_ref[rows, heads * HEAD :] = packed.astype(jnp.bfloat16)


def merge_kernel(dead_ref, own_ref, stat_ref, msg_ref, *rest, heads):
    out_ref = rest[-1]
    dead = dead_ref[pl.program_id(0)]

    @pl.when(dead == 1)
    def _():
        out_ref[...] = own_ref[...]

    @pl.when(dead == 0)
    def _():
        mine = stat_ref[...]
        parts = msg_ref[:, heads * HEAD :].astype(jnp.float32)
        other = parts + pltpu.roll(parts, HEAD - 2 * LANES, 1)
        other = other + pltpu.roll(parts, HEAD - 4 * LANES, 1)
        most = jnp.maximum(mine, other)
        mine_w = pltpu.roll(mine, HEAD - LANES, 1) * jnp.exp2(mine - most)
        other_w = pltpu.roll(other, HEAD - LANES, 1) * jnp.exp2(other - most)
        inverse = 1.0 / (mine_w + other_w)
        mine_w, other_w = mine_w * inverse, other_w * inverse
        for head in range(heads):
            columns = slice(head * HEAD, (head + 1) * HEAD)
            result = own_ref[:, columns].astype(jnp.float32) * mine_w[:, head : head + 1]
            result = result + msg_ref[:, columns].astype(jnp.float32) * other_w[:, head : head + 1]
            out_ref[:, columns] = result.astype(out_ref.dtype)


def after(value, *done):
    return lax.optimization_barrier((value, *done))[0]


def local(queries, key_values, neighbours, clean_section):
    tok_dev, feat = queries.shape[1:]
    tiles = tok_dev // TILE
    listed = neighbours.shape[1]
    heads = feat // HEAD
    cycle = lax.axis_size("tile")
    here = lax.axis_index("tile")
    section = lax.axis_index("section")
    scale = HEAD ** (-0.5) * LOG2E

    query = queries[0]
    own = key_values[:, 0]
    dead = (clean_section == section).astype(jnp.int32)
    device = neighbours // tiles
    region = jnp.where(device == here, 0, jnp.where(device == here + 1 - 2 * (here % 2), 1, 2))
    slots = (region * tiles + neighbours % tiles).reshape(-1)

    even_pairs = [(i, i ^ 1) for i in range(cycle)]
    odd_pairs = [(i, (i + 1) % cycle if i % 2 else (i - 1) % cycle) for i in range(cycle)]
    swap = [(0, 1), (1, 0)]

    sizes = group_sizes(heads)
    starts = [sum(sizes[:g]) for g in range(len(sizes))]
    odd, partner = [], []
    even = None
    for g, (start, size) in enumerate(zip(starts, sizes)):
        low, high = start * HEAD, (start + size) * HEAD
        block, ask = own[:, :, low:high], query[:, low:high]
        if g >= DEPTH:
            block, odd[g - DEPTH] = lax.optimization_barrier((block, odd[g - DEPTH]))
            ask, partner[g - DEPTH] = lax.optimization_barrier((ask, partner[g - DEPTH]))
        odd.append(lax.ppermute(block, "tile", odd_pairs))
        partner.append(lax.ppermute(ask, "section", swap))
        if even is None:
            even = lax.ppermute(own, "tile", even_pairs)

    def rows4(x):
        return x.reshape(2, tiles, TILE, x.shape[-1])

    def attend(start, size, odd_part, partner_part, slots):
        units = size * tiles * 2 * TILE * listed * TILE
        return pl.pallas_call(
            functools.partial(
                attend_kernel, tiles=tiles, listed=listed, heads=size, start=start, scale=scale
            ),
            grid_spec=pltpu.PrefetchScalarGridSpec(
                num_scalar_prefetch=2,
                grid=(size,),
                in_specs=[
                    pl.BlockSpec((tok_dev, HEAD), lambda h, *_: (0, start + h)),
                    pl.BlockSpec((tok_dev, HEAD), lambda h, *_: (0, h)),
                ]
                + [pl.BlockSpec(memory_space=pl.ANY)] * 3,
                out_specs=[
                    pl.BlockSpec((tok_dev, HEAD), lambda h, *_: (0, h)),
                    pl.BlockSpec((tok_dev, HEAD), lambda h, *_: (0, 0)),
                    pl.BlockSpec((tok_dev, (size + 1) * HEAD), lambda h, *_: (0, 0)),
                ],
                scratch_shapes=[
                    pltpu.VMEM((2, 2, 3 * tiles, TILE, HEAD), jnp.bfloat16),
                    pltpu.VMEM((2, 2 * TILE, listed * TILE), jnp.float32),
                    pltpu.SemaphoreType.DMA((2, 3)),
                ],
            ),
            out_shape=[
                jax.ShapeDtypeStruct((tok_dev, size * HEAD), jnp.bfloat16),
                jax.ShapeDtypeStruct((tok_dev, HEAD), jnp.float32),
                jax.ShapeDtypeStruct((tok_dev, (size + 1) * HEAD), jnp.bfloat16),
            ],
            cost_estimate=pl.CostEstimate(
                flops=4 * units * HEAD, transcendentals=units,
                bytes_accessed=size * HEAD * tok_dev * 2 * 10,
            ),
            compiler_params=pltpu.CompilerParams(
                dimension_semantics=("arbitrary",), vmem_limit_bytes=24 << 20
            ),
            name="attend",
        )(slots, dead, query, partner_part, rows4(own), rows4(even), rows4(odd_part))

    def merge(start, size, mine, stats, message, target):
        last = [] if target is None else [target]
        return pl.pallas_call(
            functools.partial(merge_kernel, heads=size),
            grid_spec=pltpu.PrefetchScalarGridSpec(
                num_scalar_prefetch=1,
                grid=(tiles,),
                in_specs=[
                    pl.BlockSpec((TILE, size * HEAD), lambda t, *_: (t, 0)),
                    pl.BlockSpec((TILE, HEAD), lambda t, *_: (t, 0)),
                    pl.BlockSpec((TILE, (size + 1) * HEAD), lambda t, *_: (t, 0)),
                ]
                + [pl.BlockSpec(memory_space=pl.ANY)] * len(last),
                out_specs=pl.BlockSpec((TILE, size * HEAD), lambda t, *_: (t, start // size)),
            ),
            out_shape=jax.ShapeDtypeStruct((tok_dev, feat), jnp.bfloat16),
            input_output_aliases={4: 0} if last else {},
            cost_estimate=pl.CostEstimate(
                flops=size * HEAD * tok_dev * 8, transcendentals=0,
                bytes_accessed=size * HEAD * tok_dev * 2 * 3,
            ),
            compiler_params=pltpu.CompilerParams(
                dimension_semantics=("arbitrary",), vmem_limit_bytes=16 << 20
            ),
            name="merge",
        )(dead, mine, stats, message, *last)

    target = None
    waiting = []
    for g, (start, size) in enumerate(zip(starts, sizes)):
        index = slots
        if len(waiting) >= LAG:
            target = merge(*waiting.pop(0), target)
            index, target = lax.optimization_barrier((slots, target))
        mine, stats, message = attend(start, size, odd[g], partner[g], index)
        waiting.append((start, size, mine, stats, lax.ppermute(message, "section", swap)))
    for item in waiting:
        target = merge(*item, target)
    return target[None]


def solution(mesh):
    placed = (
        P("section", "tile", None),
        P(None, "section", "tile", None),
        P("tile", None),
        P("tile"),
    )
    return jax.shard_map(
        local, mesh=mesh, in_specs=placed, out_specs=P("section", "tile", None), check_vma=False
    )
```

```python
import functools
import math

import jax
import jax.numpy as jnp
from jax import lax
from jax.experimental import pallas as pl
from jax.experimental.pallas import tpu as pltpu
from jax.sharding import PartitionSpec as P

HEAD = 128
TILE = 128
LOG2E = math.log2(math.e)
MASKED = -1e30 * LOG2E
LOWEST = -3e38
SPAN = 4
LANES = 16
SIZES = (4, 4, 8, 8)
ASKS = (4, 4, 16)
MERGES = {2: 1, 3: 1}
DEPTH = 2


def group_sizes(heads):
    if sum(SIZES) == heads:
        return SIZES
    return (4,) * (heads // 4) + (1,) * (heads % 4)


def ask_sizes(heads):
    return ASKS if sum(ASKS) == heads else (heads,)


def parts_of(x):
    hi = x.astype(jnp.bfloat16).astype(jnp.float32)
    rest = x - hi
    mid = rest.astype(jnp.bfloat16).astype(jnp.float32)
    return hi, mid, rest - mid


def attend_kernel(
    slots_ref, dead_ref, q_ref, qp_ref, own_ref, even_ref, odd_ref,
    out_ref, stat_ref, msg_ref, windows, scores, sems,
    *, tiles, listed, heads, start, scale,
):
    head = pl.program_id(0)
    slot = head % 2
    columns = pl.ds(pl.multiple_of(head * HEAD, HEAD), HEAD)
    lane = lax.broadcasted_iota(jnp.int32, (TILE, HEAD), 1)
    own_row = lax.broadcasted_iota(jnp.int32, (2 * TILE, 1), 0) < TILE
    count = listed // SPAN
    wide = SPAN * TILE

    def copies(which):
        for region, ref in enumerate((own_ref, even_ref, odd_ref)):
            first = (start + which if region == 1 else which) * HEAD
            yield pltpu.make_async_copy(
                ref.at[:, :, :, pl.ds(pl.multiple_of(first, HEAD), HEAD)],
                windows.at[which % 2, :, region * tiles : (region + 1) * tiles],
                sems.at[which % 2, region],
            )

    @pl.when(head == 0)
    def _():
        for copy in copies(head):
            copy.start()
        stat_ref[...] = jnp.zeros_like(stat_ref)

    @pl.when(head + 1 < heads)
    def _():
        for copy in copies(head + 1):
            copy.start()

    for copy in copies(head):
        copy.wait()

    def rows_of(tile):
        return slice(tile * TILE, (tile + 1) * TILE)

    def gathered(kind, tile, index):
        first = tile * listed + SPAN * index
        return jnp.concatenate(
            [windows[slot, kind, slots_ref[first + k]] for k in range(SPAN)], 0
        )

    def score(tile, index, query, running):
        part = lax.dot_general(
            query, gathered(0, tile, index), (((1,), (1,)), ((), ())),
            preferred_element_type=jnp.float32,
        )
        scores[tile % 2, :, wide * index : wide * (index + 1)] = part
        for k in range(SPAN):
            piece = part[:, k * TILE : (k + 1) * TILE]
            running = piece if running is None else jnp.maximum(running, piece)
        return running

    def query_of(tile):
        return jnp.concatenate([q_ref[rows_of(tile), :], qp_ref[rows_of(tile), :]], 0)

    running = None
    query = query_of(0)
    for index in range(count):
        running = score(0, index, query, running)
    for tile in range(tiles):
        rows = rows_of(tile)
        floor = jnp.where(own_row & (dead_ref[tile] == 1), MASKED, LOWEST)
        top = jnp.maximum(jnp.max(running, axis=1, keepdims=True) * scale, floor)
        extra = jnp.where(floor == LOWEST, 0.0, jnp.exp2(floor - top))
        running, total, acc = None, None, None
        if tile + 1 < tiles:
            query = query_of(tile + 1)
        for index in range(count):
            if tile + 1 < tiles:
                running = score(tile + 1, index, query, running)
            part = scores[tile % 2, :, wide * index : wide * (index + 1)]
            weight = jnp.exp2(part * scale - top) + extra
            for k in range(SPAN):
                piece = weight[:, k * TILE : (k + 1) * TILE]
                total = piece if total is None else total + piece
            term = jnp.dot(
                weight.astype(jnp.bfloat16), gathered(1, tile, index),
                preferred_element_type=jnp.float32,
            )
            acc = term if acc is None else acc + term
        total = jnp.sum(total, axis=1, keepdims=True)
        result = (acc * (1.0 / total)).astype(jnp.bfloat16)
        out_ref[rows, :] = result[:TILE]
        msg_ref[rows, columns] = result[TILE:]
        stats = stat_ref[rows, :]
        for k, value in enumerate((top[:TILE], total[:TILE], top[TILE:], total[TILE:])):
            stats = jnp.where(lane == head + LANES * k, value, stats)
        stat_ref[rows, :] = stats

    @pl.when(head == heads - 1)
    def _():
        for tile in range(tiles):
            rows = rows_of(tile)
            packed = jnp.zeros((TILE, HEAD), jnp.float32)
            for k, value in enumerate(parts_of(stat_ref[rows, :])):
                moved = pltpu.roll(value, (HEAD - 2 * LANES + 2 * LANES * k) % HEAD, 1)
                packed = jnp.where(lane // (2 * LANES) == k, moved, packed)
            msg_ref[rows, heads * HEAD :] = packed.astype(jnp.bfloat16)


def merge_kernel(dead_ref, own_ref, stat_ref, msg_ref, *rest, heads):
    out_ref = rest[-1]
    dead = dead_ref[pl.program_id(0)]

    @pl.when(dead == 1)
    def _():
        out_ref[...] = own_ref[...]

    @pl.when(dead == 0)
    def _():
        mine = stat_ref[...]
        parts = msg_ref[:, heads * HEAD :].astype(jnp.float32)
        other = parts + pltpu.roll(parts, HEAD - 2 * LANES, 1)
        other = other + pltpu.roll(parts, HEAD - 4 * LANES, 1)
        most = jnp.maximum(mine, other)
        mine_w = pltpu.roll(mine, HEAD - LANES, 1) * jnp.exp2(mine - most)
        other_w = pltpu.roll(other, HEAD - LANES, 1) * jnp.exp2(other - most)
        inverse = 1.0 / (mine_w + other_w)
        mine_w, other_w = mine_w * inverse, other_w * inverse
        for head in range(heads):
            columns = slice(head * HEAD, (head + 1) * HEAD)
            result = own_ref[:, columns].astype(jnp.float32) * mine_w[:, head : head + 1]
            result = result + msg_ref[:, columns].astype(jnp.float32) * other_w[:, head : head + 1]
            out_ref[:, columns] = result.astype(out_ref.dtype)


def local(queries, key_values, neighbours, clean_section):
    tok_dev, feat = queries.shape[1:]
    tiles = tok_dev // TILE
    listed = neighbours.shape[1]
    heads = feat // HEAD
    cycle = lax.axis_size("tile")
    here = lax.axis_index("tile")
    section = lax.axis_index("section")
    scale = HEAD ** (-0.5) * LOG2E

    query = queries[0]
    own = key_values[:, 0]
    dead = (clean_section == section).astype(jnp.int32)
    device = neighbours // tiles
    region = jnp.where(device == here, 0, jnp.where(device == here + 1 - 2 * (here % 2), 1, 2))
    slots = (region * tiles + neighbours % tiles).reshape(-1)

    even_pairs = [(i, i ^ 1) for i in range(cycle)]
    odd_pairs = [(i, (i + 1) % cycle if i % 2 else (i - 1) % cycle) for i in range(cycle)]
    swap = [(0, 1), (1, 0)]

    sizes = group_sizes(heads)
    starts = [sum(sizes[:g]) for g in range(len(sizes))]
    groups = range(len(sizes))
    cuts = [own[:, :, starts[g] * HEAD : (starts[g] + sizes[g]) * HEAD] for g in groups]
    blocks, odd = [], []

    def send(block):
        blocks.append(block)
        odd.append(lax.ppermute(block, "tile", odd_pairs))

    for g in range(DEPTH):
        send(cuts[g])
    even = lax.ppermute(own, "tile", even_pairs)

    partner = []
    first = 0
    for g, size in enumerate(ask_sizes(heads)):
        ask = query[:, first * HEAD : (first + size) * HEAD]
        if g >= DEPTH:
            *held, moved = partner[g - DEPTH]
            ask, moved = lax.optimization_barrier((ask, moved))
            partner[g - DEPTH] = (*held, moved)
        partner.append((first, size, lax.ppermute(ask, "section", swap)))
        first += size

    def partner_of(start):
        for first, size, moved in partner:
            if first <= start < first + size:
                return start - first, moved

    def rows4(x):
        return x.reshape(2, tiles, TILE, x.shape[-1])

    def attend(start, size, own_part, odd_part, slots):
        skip, asked = partner_of(start)
        units = size * tiles * 2 * TILE * listed * TILE
        return pl.pallas_call(
            functools.partial(
                attend_kernel, tiles=tiles, listed=listed, heads=size, start=start, scale=scale
            ),
            grid_spec=pltpu.PrefetchScalarGridSpec(
                num_scalar_prefetch=2,
                grid=(size,),
                in_specs=[
                    pl.BlockSpec((tok_dev, HEAD), lambda h, *_: (0, start + h)),
                    pl.BlockSpec((tok_dev, HEAD), lambda h, *_: (0, skip + h)),
                ]
                + [pl.BlockSpec(memory_space=pl.ANY)] * 3,
                out_specs=[
                    pl.BlockSpec((tok_dev, HEAD), lambda h, *_: (0, h)),
                    pl.BlockSpec((tok_dev, HEAD), lambda h, *_: (0, 0)),
                    pl.BlockSpec((tok_dev, (size + 1) * HEAD), lambda h, *_: (0, 0)),
                ],
                scratch_shapes=[
                    pltpu.VMEM((2, 2, 3 * tiles, TILE, HEAD), jnp.bfloat16),
                    pltpu.VMEM((2, 2 * TILE, listed * TILE), jnp.float32),
                    pltpu.SemaphoreType.DMA((2, 3)),
                ],
            ),
            out_shape=[
                jax.ShapeDtypeStruct((tok_dev, size * HEAD), jnp.bfloat16),
                jax.ShapeDtypeStruct((tok_dev, HEAD), jnp.float32),
                jax.ShapeDtypeStruct((tok_dev, (size + 1) * HEAD), jnp.bfloat16),
            ],
            cost_estimate=pl.CostEstimate(
                flops=4 * units * HEAD, transcendentals=units,
                bytes_accessed=size * HEAD * tok_dev * 2 * 10,
            ),
            compiler_params=pltpu.CompilerParams(
                dimension_semantics=("arbitrary",), vmem_limit_bytes=24 << 20
            ),
            name="attend",
        )(slots, dead, query, asked, rows4(own_part), rows4(even), rows4(odd_part))

    def merge(start, size, mine, stats, message, target):
        last = [] if target is None else [target]
        return pl.pallas_call(
            functools.partial(merge_kernel, heads=size),
            grid_spec=pltpu.PrefetchScalarGridSpec(
                num_scalar_prefetch=1,
                grid=(tiles,),
                in_specs=[
                    pl.BlockSpec((TILE, size * HEAD), lambda t, *_: (t, 0)),
                    pl.BlockSpec((TILE, HEAD), lambda t, *_: (t, 0)),
                    pl.BlockSpec((TILE, (size + 1) * HEAD), lambda t, *_: (t, 0)),
                ]
                + [pl.BlockSpec(memory_space=pl.ANY)] * len(last),
                out_specs=pl.BlockSpec((TILE, size * HEAD), lambda t, *_: (t, start // size)),
            ),
            out_shape=jax.ShapeDtypeStruct((tok_dev, feat), jnp.bfloat16),
            input_output_aliases={4: 0} if last else {},
            cost_estimate=pl.CostEstimate(
                flops=size * HEAD * tok_dev * 8, transcendentals=0,
                bytes_accessed=size * HEAD * tok_dev * 2 * 3,
            ),
            compiler_params=pltpu.CompilerParams(
                dimension_semantics=("arbitrary",), vmem_limit_bytes=24 << 20
            ),
            name="merge",
        )(dead, mine, stats, message, *last)

    target = None
    waiting = []
    for g, (start, size) in enumerate(zip(starts, sizes)):
        index = slots
        if g:
            index, stats = lax.optimization_barrier((index, waiting[-1][3]))
            waiting[-1][3] = stats
        for _ in range(MERGES.get(g, 0) if len(sizes) == len(SIZES) else 0):
            target = merge(*waiting.pop(0), target)
            index, target = lax.optimization_barrier((index, target))
        if g + DEPTH < len(sizes):
            block, odd[g] = lax.optimization_barrier((cuts[g + DEPTH], odd[g]))
            if g:
                block, waiting[-1][3] = lax.optimization_barrier((block, waiting[-1][3]))
            send(block)
        mine, stats, message = attend(start, size, blocks[g], odd[g], index)
        waiting.append([start, size, mine, stats, lax.ppermute(message, "section", swap)])
    for item in waiting:
        target = merge(*item, target)
    return target[None]


def solution(mesh):
    placed = (
        P("section", "tile", None),
        P(None, "section", "tile", None),
        P("tile", None),
        P("tile"),
    )
    return jax.shard_map(
        local, mesh=mesh, in_specs=placed, out_specs=P("section", "tile", None), check_vma=False
    )
```

```python
import functools
import math

import jax
import jax.numpy as jnp
from jax import lax
from jax.experimental import pallas as pl
from jax.experimental.pallas import tpu as pltpu
from jax.sharding import PartitionSpec as P

HEAD = 128
TILE = 128
LOG2E = math.log2(math.e)
MASKED = -1e30 * LOG2E
LOWEST = -3e38
SPAN = 4
LANES = 16
SIZES = (4, 4, 8, 8)
ASKS = (4, 4, 16)
MERGES = {2: 1, 3: 1}
DEPTH = 2


def group_sizes(heads):
    if sum(SIZES) == heads:
        return SIZES
    return (4,) * (heads // 4) + (1,) * (heads % 4)


def ask_sizes(heads):
    return ASKS if sum(ASKS) == heads else (heads,)


def parts_of(x):
    hi = x.astype(jnp.bfloat16).astype(jnp.float32)
    rest = x - hi
    mid = rest.astype(jnp.bfloat16).astype(jnp.float32)
    return hi, mid, rest - mid


def attend_kernel(
    slots_ref, dead_ref, q_ref, qp_ref, own_ref, even_ref, odd_ref,
    out_ref, stat_ref, msg_ref, windows, scores, sems,
    *, tiles, listed, heads, start, scale,
):
    head = pl.program_id(0)
    slot = head % 2
    columns = pl.ds(pl.multiple_of(head * HEAD, HEAD), HEAD)
    lane = lax.broadcasted_iota(jnp.int32, (TILE, HEAD), 1)
    own_row = lax.broadcasted_iota(jnp.int32, (2 * TILE, 1), 0) < TILE
    count = listed // SPAN
    wide = SPAN * TILE

    def copies(which):
        for region, ref in enumerate((own_ref, even_ref, odd_ref)):
            first = (start + which if region == 1 else which) * HEAD
            yield pltpu.make_async_copy(
                ref.at[:, :, :, pl.ds(pl.multiple_of(first, HEAD), HEAD)],
                windows.at[which % 2, :, region * tiles : (region + 1) * tiles],
                sems.at[which % 2, region],
            )

    @pl.when(head == 0)
    def _():
        for copy in copies(head):
            copy.start()
        stat_ref[...] = jnp.zeros_like(stat_ref)

    @pl.when(head + 1 < heads)
    def _():
        for copy in copies(head + 1):
            copy.start()

    for copy in copies(head):
        copy.wait()

    def rows_of(tile):
        return slice(tile * TILE, (tile + 1) * TILE)

    def gathered(kind, tile, index):
        first = tile * listed + SPAN * index
        return jnp.concatenate(
            [windows[slot, kind, slots_ref[first + k]] for k in range(SPAN)], 0
        )

    def score(tile, index, query, running):
        part = lax.dot_general(
            query, gathered(0, tile, index), (((1,), (1,)), ((), ())),
            preferred_element_type=jnp.float32,
        )
        scores[tile % 2, :, wide * index : wide * (index + 1)] = part
        for k in range(SPAN):
            piece = part[:, k * TILE : (k + 1) * TILE]
            running = piece if running is None else jnp.maximum(running, piece)
        return running

    def query_of(tile):
        return jnp.concatenate([q_ref[rows_of(tile), :], qp_ref[rows_of(tile), :]], 0)

    running = None
    query = query_of(0)
    for index in range(count):
        running = score(0, index, query, running)
    for tile in range(tiles):
        rows = rows_of(tile)
        floor = jnp.where(own_row & (dead_ref[tile] == 1), MASKED, LOWEST)
        top = jnp.maximum(jnp.max(running, axis=1, keepdims=True) * scale, floor)
        extra = jnp.where(floor == LOWEST, 0.0, jnp.exp2(floor - top))
        running, total, acc = None, None, None
        if tile + 1 < tiles:
            query = query_of(tile + 1)
        for index in range(count):
            if tile + 1 < tiles:
                running = score(tile + 1, index, query, running)
            part = scores[tile % 2, :, wide * index : wide * (index + 1)]
            weight = jnp.exp2(part * scale - top) + extra
            for k in range(SPAN):
                piece = weight[:, k * TILE : (k + 1) * TILE]
                total = piece if total is None else total + piece
            term = jnp.dot(
                weight.astype(jnp.bfloat16), gathered(1, tile, index),
                preferred_element_type=jnp.float32,
            )
            acc = term if acc is None else acc + term
        total = jnp.sum(total, axis=1, keepdims=True)
        result = (acc * (1.0 / total)).astype(jnp.bfloat16)
        out_ref[rows, :] = result[:TILE]
        msg_ref[rows, columns] = result[TILE:]
        stats = stat_ref[rows, :]
        for k, value in enumerate((top[:TILE], total[:TILE], top[TILE:], total[TILE:])):
            stats = jnp.where(lane == head + LANES * k, value, stats)
        stat_ref[rows, :] = stats

    @pl.when(head == heads - 1)
    def _():
        for tile in range(tiles):
            rows = rows_of(tile)
            packed = jnp.zeros((TILE, HEAD), jnp.float32)
            for k, value in enumerate(parts_of(stat_ref[rows, :])):
                moved = pltpu.roll(value, (HEAD - 2 * LANES + 2 * LANES * k) % HEAD, 1)
                packed = jnp.where(lane // (2 * LANES) == k, moved, packed)
            msg_ref[rows, heads * HEAD :] = packed.astype(jnp.bfloat16)


def merge_kernel(dead_ref, own_ref, stat_ref, msg_ref, *rest, heads):
    out_ref = rest[-1]
    dead = dead_ref[pl.program_id(0)]

    @pl.when(dead == 1)
    def _():
        out_ref[...] = own_ref[...]

    @pl.when(dead == 0)
    def _():
        mine = stat_ref[...]
        parts = msg_ref[:, heads * HEAD :].astype(jnp.float32)
        other = parts + pltpu.roll(parts, HEAD - 2 * LANES, 1)
        other = other + pltpu.roll(parts, HEAD - 4 * LANES, 1)
        most = jnp.maximum(mine, other)
        mine_w = pltpu.roll(mine, HEAD - LANES, 1) * jnp.exp2(mine - most)
        other_w = pltpu.roll(other, HEAD - LANES, 1) * jnp.exp2(other - most)
        inverse = 1.0 / (mine_w + other_w)
        mine_w, other_w = mine_w * inverse, other_w * inverse
        for head in range(heads):
            columns = slice(head * HEAD, (head + 1) * HEAD)
            result = own_ref[:, columns].astype(jnp.float32) * mine_w[:, head : head + 1]
            result = result + msg_ref[:, columns].astype(jnp.float32) * other_w[:, head : head + 1]
            out_ref[:, columns] = result.astype(out_ref.dtype)


def local(queries, key_values, neighbours, clean_section):
    tok_dev, feat = queries.shape[1:]
    tiles = tok_dev // TILE
    listed = neighbours.shape[1]
    heads = feat // HEAD
    cycle = lax.axis_size("tile")
    here = lax.axis_index("tile")
    section = lax.axis_index("section")
    scale = HEAD ** (-0.5) * LOG2E

    query = queries[0]
    own = key_values[:, 0]
    dead = (clean_section == section).astype(jnp.int32)
    device = neighbours // tiles
    region = jnp.where(device == here, 0, jnp.where(device == here + 1 - 2 * (here % 2), 1, 2))
    slots = (region * tiles + neighbours % tiles).reshape(-1)

    even_pairs = [(i, i ^ 1) for i in range(cycle)]
    odd_pairs = [(i, (i + 1) % cycle if i % 2 else (i - 1) % cycle) for i in range(cycle)]
    swap = [(0, 1), (1, 0)]

    sizes = group_sizes(heads)
    starts = [sum(sizes[:g]) for g in range(len(sizes))]
    groups = range(len(sizes))
    cuts = [own[:, :, starts[g] * HEAD : (starts[g] + sizes[g]) * HEAD] for g in groups]
    blocks, odd = [], []

    def send(block):
        blocks.append(block)
        odd.append(lax.ppermute(block, "tile", odd_pairs))

    for g in range(DEPTH):
        send(cuts[g])
    even = lax.ppermute(own, "tile", even_pairs)

    partner = []
    first = 0
    for g, size in enumerate(ask_sizes(heads)):
        ask = query[:, first * HEAD : (first + size) * HEAD]
        if g >= DEPTH:
            *held, moved = partner[g - DEPTH]
            ask, moved = lax.optimization_barrier((ask, moved))
            partner[g - DEPTH] = (*held, moved)
        partner.append((first, size, lax.ppermute(ask, "section", swap)))
        first += size

    def partner_of(start):
        for first, size, moved in partner:
            if first <= start < first + size:
                return start - first, moved

    def rows4(x):
        return x.reshape(2, tiles, TILE, x.shape[-1])

    def attend(start, size, own_part, odd_part, slots):
        skip, asked = partner_of(start)
        units = size * tiles * 2 * TILE * listed * TILE
        return pl.pallas_call(
            functools.partial(
                attend_kernel, tiles=tiles, listed=listed, heads=size, start=start, scale=scale
            ),
            grid_spec=pltpu.PrefetchScalarGridSpec(
                num_scalar_prefetch=2,
                grid=(size,),
                in_specs=[
                    pl.BlockSpec((tok_dev, HEAD), lambda h, *_: (0, start + h)),
                    pl.BlockSpec((tok_dev, HEAD), lambda h, *_: (0, skip + h)),
                ]
                + [pl.BlockSpec(memory_space=pl.ANY)] * 3,
                out_specs=[
                    pl.BlockSpec((tok_dev, HEAD), lambda h, *_: (0, h)),
                    pl.BlockSpec((tok_dev, HEAD), lambda h, *_: (0, 0)),
                    pl.BlockSpec((tok_dev, (size + 1) * HEAD), lambda h, *_: (0, 0)),
                ],
                scratch_shapes=[
                    pltpu.VMEM((2, 2, 3 * tiles, TILE, HEAD), jnp.bfloat16),
                    pltpu.VMEM((2, 2 * TILE, listed * TILE), jnp.float32),
                    pltpu.SemaphoreType.DMA((2, 3)),
                ],
            ),
            out_shape=[
                jax.ShapeDtypeStruct((tok_dev, size * HEAD), jnp.bfloat16),
                jax.ShapeDtypeStruct((tok_dev, HEAD), jnp.float32),
                jax.ShapeDtypeStruct((tok_dev, (size + 1) * HEAD), jnp.bfloat16),
            ],
            cost_estimate=pl.CostEstimate(
                flops=4 * units * HEAD, transcendentals=units,
                bytes_accessed=size * HEAD * tok_dev * 2 * 10,
            ),
            compiler_params=pltpu.CompilerParams(
                dimension_semantics=("arbitrary",), vmem_limit_bytes=24 << 20
            ),
            name="attend",
        )(slots, dead, query, asked, rows4(own_part), rows4(even), rows4(odd_part))

    def merge(start, size, mine, stats, message, target):
        last = [] if target is None else [target]
        return pl.pallas_call(
            functools.partial(merge_kernel, heads=size),
            grid_spec=pltpu.PrefetchScalarGridSpec(
                num_scalar_prefetch=1,
                grid=(tiles,),
                in_specs=[
                    pl.BlockSpec((TILE, size * HEAD), lambda t, *_: (t, 0)),
                    pl.BlockSpec((TILE, HEAD), lambda t, *_: (t, 0)),
                    pl.BlockSpec((TILE, (size + 1) * HEAD), lambda t, *_: (t, 0)),
                ]
                + [pl.BlockSpec(memory_space=pl.ANY)] * len(last),
                out_specs=pl.BlockSpec((TILE, size * HEAD), lambda t, *_: (t, start // size)),
            ),
            out_shape=jax.ShapeDtypeStruct((tok_dev, feat), jnp.bfloat16),
            input_output_aliases={4: 0} if last else {},
            cost_estimate=pl.CostEstimate(
                flops=size * HEAD * tok_dev * 8, transcendentals=0,
                bytes_accessed=size * HEAD * tok_dev * 2 * 3,
            ),
            compiler_params=pltpu.CompilerParams(
                dimension_semantics=("arbitrary",), vmem_limit_bytes=24 << 20
            ),
            name="merge",
        )(dead, mine, stats, message, *last)

    target = None
    waiting = []
    pace = jnp.zeros((8, HEAD), jnp.float32)
    for g, (start, size) in enumerate(zip(starts, sizes)):
        index = slots
        if g:
            index, stats = lax.optimization_barrier((index, waiting[-1][3]))
            waiting[-1][3] = stats
        for _ in range(MERGES.get(g, 0) if len(sizes) == len(SIZES) else 0):
            target = merge(*waiting.pop(0), target)
            index, target = lax.optimization_barrier((index, target))
        if g + DEPTH < len(sizes):
            pace, odd[g] = lax.optimization_barrier((pace, odd[g]))
            pace = lax.ppermute(pace, "tile", even_pairs)
            block = cuts[g + DEPTH]
            if g:
                block, pace, waiting[-1][3] = lax.optimization_barrier((block, pace, waiting[-1][3]))
            else:
                block, pace = lax.optimization_barrier((block, pace))
            send(block)
        mine, stats, message = attend(start, size, blocks[g], odd[g], index)
        waiting.append([start, size, mine, stats, lax.ppermute(message, "section", swap)])
    for item in waiting:
        target = merge(*item, target)
    return target[None]


def solution(mesh):
    placed = (
        P("section", "tile", None),
        P(None, "section", "tile", None),
        P("tile", None),
        P("tile"),
    )
    return jax.shard_map(
        local, mesh=mesh, in_specs=placed, out_specs=P("section", "tile", None), check_vma=False
    )
```
